128 devices in a mesh: dp: 2 (over core), row: 8 (over y, x_hi), col: 8 (over z, x_lo).
Axes of the slice: x: 4 (x_hi: 2, x_lo: 2; x = x_hi * 2 + x_lo), y: 4, z: 4, core: 2. Of those that a mesh axis runs over, the one named last changes fastest.
Arguments:
- context: bfloat16 [2048, 8192], P(('dp', 'col'), 'row'), may hold values from -6 to 6
- out_weight: bfloat16 [8192, 8192], P('row', 'col'), may hold values from -0.0625 to 0.0625
- up_weight: bfloat16 [8192, 14336], P('col', 'row'), may hold values from -0.0625 to 0.0625
- down_weight: bfloat16 [14336, 8192], P('row', 'col'), may hold values from -0.046875 to 0.046875
- cotangent: bfloat16 [2048, 8192], P(('dp', 'row'), 'col'), may hold values from -6 to 6
- masked_pos: int32 [16, 20], P(('dp', 'row')), may hold values from 0 to 127, as said below
Outputs:
- block_out: bfloat16 [2048, 8192], P(('dp', 'row'), 'col')
- context_grad: bfloat16 [2048, 8192], P(('dp', 'col'), 'row')
- out_grad: bfloat16 [8192, 8192], P('row', 'col')
- up_grad: bfloat16 [8192, 14336], P('col', 'row')
- down_grad: bfloat16 [14336, 8192], P('row', 'col')
The draws below stay inside these ranges and needn't reach their ends.
Inputs may be any that keep to these rules, and one draw needn't show every extreme that they name: `masked_pos`: each row names 20 different token positions of one sequence.
All inputs are finite; a program needn't handle non-finite values.
Results may differ from the reference program's by a relative error of at most 0.035.
Values may be sent and summed in bfloat16 or wider, within the bound.
No kernel may reach another device: no remote copies, remote signals or barrier semaphores. Data moves between devices by JAX's collectives and lax.ppermute only.
A program may use at most 192 MiB of HBM per device.

```python
import jax
import jax.numpy as jnp
from jax import lax

D = 8192
FF = 14336
SEQ = 128
MASKED = 20
TOKENS = 2048
SEQS = 16
N_DP = 2
N_ROW = 8
N_COL = 8


def draw_masked_pos(key, part):
    scores = jax.random.randint(key, (SEQS, SEQ), 0, 1048576) * SEQ + jnp.arange(SEQ, dtype=jnp.int32)[None, :]
    order = jnp.argsort(scores, axis=1, stable=True)
    return order[:, :MASKED].astype(jnp.int32)


def levels(stream_key, shape, pieces, low, top_value):
    loudness = 1.0
    for position, blocks in pieces:
        heights = jax.random.uniform(jax.random.fold_in(jax.random.fold_in(stream_key, 6), position), (blocks,), jnp.float32, low / len(pieces), top_value / len(pieces))
        loudness = loudness * jnp.repeat(jnp.exp(heights), shape[position] // blocks).reshape((-1,) + (1,) * (len(shape) - 1 - position))
    return loudness


def normal_values(own_key, shape, spread, bound, cuts=(), held_as=jnp.bfloat16):
    entries = spread * jax.random.normal(own_key, shape, jnp.float32)
    if cuts:
        entries = entries * levels(own_key, shape, cuts, -0.22, 0.18)
    return jnp.clip(entries, -bound, bound).astype(held_as)


def setup_inputs(seed: int = 0) -> dict:
    key_list = jax.random.split(jax.random.key(seed), 7)
    context = normal_values(key_list[0], (TOKENS, D), 1.0, 6.0, ((0, 16), (1, 8)))
    out_weight = normal_values(key_list[1], (D, D), D ** -0.5, 0.0625, ((0, 8), (1, 8)))
    up_weight = normal_values(key_list[2], (D, FF), D ** -0.5, 0.0625, ((0, 8), (1, 8)))
    down_weight = normal_values(key_list[3], (FF, D), FF ** -0.5, 0.046875, ((0, 8), (1, 8)))
    cotangent = normal_values(key_list[4], (TOKENS, D), 1.0, 6.0, ((0, 16), (1, 8)))
    masked_pos = draw_masked_pos(jax.random.fold_in(key_list[6], 71), 0)
    return {"context": context, "out_weight": out_weight, "up_weight": up_weight, "down_weight": down_weight, "cotangent": cotangent, "masked_pos": masked_pos}


coef = 0.7978845608
cubic = 0.044715


def gelu(value):
    inner = jnp.tanh(coef * (value + cubic * value * value * value))
    return 0.5 * value * (1.0 + inner)


def gelu_slope(value):
    inner = jnp.tanh(coef * (value + cubic * value * value * value))
    return 0.5 * (1.0 + inner) + 0.5 * value * (1.0 - inner * inner) * coef * (1.0 + 3.0 * cubic * value * value)


def split_sum(left, right, count):
    width = left.shape[1] // count
    total = jnp.zeros((left.shape[0], right.shape[1]), jnp.float32)
    for index in range(count):
        term = jnp.dot(left[:, index * width:(index + 1) * width], right[index * width:(index + 1) * width], preferred_element_type=jnp.float32)
        rounded = lax.optimization_barrier(term.astype(jnp.bfloat16))
        total = total + rounded.astype(jnp.float32)
    return total


def replica_sum(left, right):
    rows_each = left.shape[0] // N_DP
    total = jnp.zeros((left.shape[1], right.shape[1]), jnp.float32)
    for index in range(N_DP):
        part_left = left[index * rows_each:(index + 1) * rows_each]
        part_right = right[index * rows_each:(index + 1) * rows_each]
        term = jnp.dot(part_left.T, part_right, preferred_element_type=jnp.float32)
        rounded = lax.optimization_barrier(term.astype(jnp.bfloat16))
        total = total + rounded.astype(jnp.float32)
    return total.astype(jnp.bfloat16)


def token_mask(masked_pos):
    places = jnp.arange(SEQ, dtype=jnp.int32)
    hits = masked_pos[:, :, None] == places[None, None, :]
    return jnp.any(hits, axis=1).astype(jnp.float32).reshape(-1)


def reference(context, out_weight, up_weight, down_weight, cotangent, masked_pos):
    projected = split_sum(context, out_weight, N_ROW).astype(jnp.bfloat16)
    pre_act = split_sum(projected, up_weight, N_COL).astype(jnp.bfloat16)
    pre_float = pre_act.astype(jnp.float32)
    act = gelu(pre_float).astype(jnp.bfloat16)
    block_out = split_sum(act, down_weight, N_ROW).astype(jnp.bfloat16)
    keep = token_mask(masked_pos)
    grad_out = (cotangent.astype(jnp.float32) * keep[:, None]).astype(jnp.bfloat16)
    grad_act = split_sum(grad_out, down_weight.T, N_COL)
    grad_hidden = (grad_act * gelu_slope(pre_float)).astype(jnp.bfloat16)
    grad_proj = split_sum(grad_hidden, up_weight.T, N_ROW).astype(jnp.bfloat16)
    context_grad = split_sum(grad_proj, out_weight.T, N_COL).astype(jnp.bfloat16)
    out_grad = replica_sum(context, grad_proj)
    up_grad = replica_sum(projected, grad_hidden)
    down_grad = replica_sum(act, grad_out)
    return (block_out, context_grad, out_grad, up_grad, down_grad)
```

```python
import jax
import jax.numpy as jnp
from jax import lax
from jax.sharding import PartitionSpec as P

SEQ = 128
MASKED = 20
HEAD = 32
GROUP = 8

coef = 0.7978845608
cubic = 0.044715


def gelu(value):
    inner = jnp.tanh(coef * (value + cubic * value * value * value))
    return 0.5 * value * (1.0 + inner)


def gelu_slope(value):
    inner = jnp.tanh(coef * (value + cubic * value * value * value))
    return 0.5 * (1.0 + inner) + 0.5 * value * (1.0 - inner * inner) * coef * (
        1.0 + 3.0 * cubic * value * value
    )


def gather(values, axis):
    rows, width = values.shape
    copies = jnp.broadcast_to(values[None], (GROUP, rows, width))
    return lax.all_to_all(copies, axis, 0, 0).reshape(GROUP * rows, width)


def scatter_sum(partial, axis):
    rows, width = partial.shape
    blocks = partial.reshape(GROUP, rows // GROUP, width)
    return jnp.sum(lax.all_to_all(blocks, axis, 0, 0).astype(jnp.float32), axis=0)


def product(left, weight, contract):
    return lax.dot_general(
        left, weight, (((1,), (contract,)), ((), ())), preferred_element_type=jnp.float32
    ).astype(jnp.bfloat16)


def select(matrix, values, contract):
    return lax.dot_general(
        matrix, values, (((contract,), (0,)), ((), ())), preferred_element_type=jnp.float32
    ).astype(jnp.bfloat16)


def selectors(positions):
    places = jnp.arange(SEQ, dtype=jnp.int32)
    index = positions.reshape(MASKED, 1)
    order = jnp.arange(MASKED, dtype=jnp.int32)[:, None]
    hit = index == places[None, :]
    masked = jnp.any(hit, axis=0)
    own = jnp.sum(jnp.where(hit, order, 0), axis=0)
    before = jnp.sum((index < places[None, :]).astype(jnp.int32), axis=0)
    slot = jnp.where(masked, own, MASKED + places - before)
    full = places[:, None] == slot[None, :]
    head = full[:HEAD] & masked[None, :]
    return full.astype(jnp.bfloat16), head.astype(jnp.bfloat16)


def forward(values, out_weight, up_weight, down_weight):
    ctx_full = gather(values, "col")
    projected = scatter_sum(product(ctx_full, out_weight, 0), "row").astype(jnp.bfloat16)
    proj_full = gather(projected, "row")
    pre_act = scatter_sum(product(proj_full, up_weight, 0), "col").astype(jnp.bfloat16)
    act = gelu(pre_act.astype(jnp.float32)).astype(jnp.bfloat16)
    act_full = gather(act, "col")
    block_out = scatter_sum(product(act_full, down_weight, 0), "row").astype(jnp.bfloat16)
    return ctx_full, proj_full, pre_act, act_full, block_out


def both_replicas(values, first):
    other = lax.ppermute(values, "dp", [(0, 1), (1, 0)])
    return jnp.concatenate(
        [jnp.where(first, values, other), jnp.where(first, other, values)], axis=0
    )


def token_product(left, right):
    return lax.dot_general(
        left, right, (((0,), (0,)), ((), ())), preferred_element_type=jnp.float32
    ).astype(jnp.bfloat16)


def body(context, out_weight, up_weight, down_weight, cotangent, masked_pos):
    crossed = [(r * GROUP + c, c * GROUP + r) for r in range(GROUP) for c in range(GROUP)]
    col_pos = lax.ppermute(masked_pos, ("row", "col"), crossed)
    row_full, row_head = selectors(masked_pos)
    col_full, col_head = selectors(col_pos)
    first = lax.axis_index("dp") == 0

    arranged = select(col_full, context, 1)
    ctx_full, proj_full, pre_act, act_full, head_out = forward(
        arranged[:HEAD], out_weight, up_weight, down_weight
    )
    grad_out = select(row_head, cotangent, 1)
    grad_full = gather(grad_out, "row")
    grad_act = scatter_sum(product(grad_full, down_weight, 1), "col")
    grad_hidden = (grad_act * gelu_slope(pre_act.astype(jnp.float32))).astype(jnp.bfloat16)
    hidden_full = gather(grad_hidden, "col")
    grad_proj = scatter_sum(product(hidden_full, up_weight, 1), "row").astype(jnp.bfloat16)
    gproj_full = gather(grad_proj, "row")
    grad_ctx = scatter_sum(product(gproj_full, out_weight, 1), "col").astype(jnp.bfloat16)
    context_grad = select(col_head, grad_ctx, 0)

    tail_out = forward(arranged[HEAD:], out_weight, up_weight, down_weight)[4]
    block_out = select(row_full, jnp.concatenate([head_out, tail_out], axis=0), 0)

    out_grad = token_product(both_replicas(ctx_full, first), both_replicas(gproj_full, first))
    up_grad = token_product(both_replicas(proj_full, first), both_replicas(hidden_full, first))
    down_grad = token_product(both_replicas(act_full, first), both_replicas(grad_full, first))
    return (block_out, context_grad, out_grad, up_grad, down_grad)


def solution(mesh):
    placed = (
        P(("dp", "col"), "row"),
        P("row", "col"),
        P("col", "row"),
        P("row", "col"),
        P(("dp", "row"), "col"),
        P(("dp", "row"), None),
    )
    return jax.shard_map(
        body,
        mesh=mesh,
        in_specs=placed,
        out_specs=(
            P(("dp", "row"), "col"),
            P(("dp", "col"), "row"),
            P("row", "col"),
            P("col", "row"),
            P("row", "col"),
        ),
        check_vma=False,
    )
```

```python
import jax
import jax.numpy as jnp
from jax import lax
from jax.sharding import PartitionSpec as P

SEQ = 128
MASKED = 20
HEAD = 24
GROUP = 8
RING = 4
RINGS = [[0, 2, 4, 6], [1, 3, 5, 7]]
PAIRS = [(i, i ^ 1) for i in range(GROUP)]
CORES = [(0, 1), (1, 0)]

coef = 0.7978845608
cubic = 0.044715


def gelu(value):
    inner = jnp.tanh(coef * (value + cubic * value * value * value))
    return 0.5 * value * (1.0 + inner)


def gelu_slope(value):
    inner = jnp.tanh(coef * (value + cubic * value * value * value))
    return 0.5 * (1.0 + inner) + 0.5 * value * (1.0 - inner * inner) * coef * (
        1.0 + 3.0 * cubic * value * value
    )


def exchange(blocks, axis):
    groups = RINGS if blocks.shape[0] == RING else None
    return lax.all_to_all(blocks, axis, 0, 0, axis_index_groups=groups)


def gather(values, axis, count=GROUP):
    return exchange(jnp.broadcast_to(values[None], (count,) + values.shape), axis)


def scatter_sum(blocks, axis):
    return jnp.sum(exchange(blocks, axis).astype(jnp.float32), axis=0)


def dot(left, right, contract):
    return lax.dot_general(
        left, right, (((1,), (contract,)), ((), ())), preferred_element_type=jnp.float32
    )


def product(left, weight, contract):
    return dot(left, weight, contract).astype(jnp.bfloat16)


def flat(blocks):
    return blocks.reshape(-1, blocks.shape[-1])


def select(matrix, values, contract):
    return lax.dot_general(
        matrix, values, (((contract,), (0,)), ((), ())), preferred_element_type=jnp.float32
    ).astype(jnp.bfloat16)


def select_each(matrix, values):
    return lax.dot_general(
        matrix, values, (((2,), (1,)), ((0,), (0,))), preferred_element_type=jnp.float32
    ).astype(jnp.bfloat16)


def heads(positions):
    places = jnp.arange(SEQ, dtype=jnp.int32)
    short = jnp.pad(
        positions,
        [(0, 0)] * (positions.ndim - 1) + [(0, HEAD - MASKED)],
        constant_values=-1,
    )
    return (short[..., None] == places).astype(jnp.bfloat16)


def neighbour_weight(weight, core, after):
    half = weight.shape[0] // 2
    mine = lax.dynamic_slice_in_dim(weight, core * half, half, 0)
    if after is not None:
        mine = lax.optimization_barrier((mine, after))[0]
    got = lax.ppermute(mine, "col", PAIRS)
    other = lax.ppermute(got, "dp", CORES)
    first = core == 0
    whole = jnp.concatenate(
        [jnp.where(first, got, other), jnp.where(first, other, got)], axis=0
    )
    return whole, got


def interleave(own, other, side):
    even = jnp.stack([own, other], axis=1)
    odd = jnp.stack([other, own], axis=1)
    return jnp.where(side == 0, even, odd).reshape(-1, own.shape[-1])


def both_replicas(values, core):
    other = lax.ppermute(values, "dp", CORES)
    first = core == 0
    return jnp.concatenate(
        [jnp.where(first, values, other), jnp.where(first, other, values)], axis=0
    )


def token_product(left, right, core):
    return lax.dot_general(
        both_replicas(left, core),
        both_replicas(right, core),
        (((0,), (0,)), ((), ())),
        preferred_element_type=jnp.float32,
    ).astype(jnp.bfloat16)


def body(context, out_weight, up_weight, down_weight, cotangent, masked_pos):
    side = lax.axis_index("col") & 1
    core = lax.axis_index("dp")
    live = jnp.arange(HEAD) < MASKED
    crossed = [(r * GROUP + c, c * GROUP + r) for r in range(GROUP) for c in range(GROUP)]
    col_pos = lax.ppermute(masked_pos, ("row", "col"), crossed)

    ctx = gather(context, "col", RING)
    out_near, got = neighbour_weight(out_weight, core, None)
    up_near, got = neighbour_weight(up_weight, core, got)
    down_near, got = neighbour_weight(down_weight, core, got)

    noted = jnp.pad(
        masked_pos.astype(jnp.bfloat16),
        [(MASKED, HEAD - MASKED - 1), (0, cotangent.shape[1] - MASKED)],
    )
    grad_full = gather(select(heads(masked_pos[0]), cotangent, 1) + noted, "row")
    positions = grad_full[:, MASKED, :MASKED].astype(jnp.int32)
    grad_full = flat(jnp.where(live[None, :, None], grad_full, jnp.zeros_like(grad_full)))
    grad_act = lax.psum_scatter(
        product(grad_full, down_weight, 1), "col", scatter_dimension=0, tiled=True
    ).astype(jnp.float32)

    eighth = (GROUP, RING * SEQ // GROUP, context.shape[1])
    proj_own = scatter_sum(product(flat(ctx), out_weight, 0).reshape(eighth), "row")
    proj_near = scatter_sum(product(flat(ctx), out_near, 0).reshape(eighth), "row")
    own_full = flat(gather(proj_own.astype(jnp.bfloat16), "row"))
    near_full = flat(gather(proj_near.astype(jnp.bfloat16), "row"))
    up_part = (dot(own_full, up_weight, 0) + dot(near_full, up_near, 0)).astype(jnp.bfloat16)
    pre_act = scatter_sum(up_part.reshape(RING, SEQ, -1), "col").astype(jnp.bfloat16)
    act = gelu(pre_act.astype(jnp.float32)).astype(jnp.bfloat16)
    col_heads = heads(col_pos[0])
    slope = gelu_slope(select(col_heads, pre_act, 1).astype(jnp.float32))
    grad_hidden = (grad_act * slope).astype(jnp.bfloat16)

    hidden_full = flat(gather(grad_hidden, "col"))
    act_full = gather(act, "col", RING)
    hidden_full, act_full = lax.optimization_barrier((hidden_full, act_full))

    grad_proj = scatter_sum(product(hidden_full, up_weight, 1).reshape(GROUP, HEAD, -1), "row")
    gproj_full = flat(gather(grad_proj.astype(jnp.bfloat16), "row"))
    grad_ctx = scatter_sum(product(gproj_full, out_weight, 1).reshape(GROUP, HEAD, -1), "col")
    context_grad = select(col_heads, grad_ctx.astype(jnp.bfloat16), 0)

    down_part = jnp.stack(
        [
            product(flat(act_full), down_weight, 0).reshape(RING, SEQ, -1),
            product(flat(act_full), down_near, 0).reshape(RING, SEQ, -1),
        ],
        axis=1,
    )
    piece = scatter_sum(down_part.reshape(GROUP, SEQ, -1), "row").astype(jnp.bfloat16)
    moved = [
        (
            (2 * y + h) * GROUP + 2 * z + x,
            (2 * y + x) * GROUP + 2 * z + (h ^ x),
        )
        for y in range(RING)
        for h in range(2)
        for z in range(RING)
        for x in range(2)
    ]
    block_out = lax.ppermute(piece, ("row", "col"), moved)

    by_side = positions.reshape(RING, 2, MASKED)
    ring_heads = heads(jnp.where(side == 0, by_side[:, 0], by_side[:, 1]))
    ctx_own = select_each(ring_heads, ctx)
    ctx_head = interleave(ctx_own, lax.ppermute(ctx_own, "col", PAIRS), side)
    proj_head = interleave(
        select_each(ring_heads, own_full.reshape(RING, SEQ, -1)),
        lax.ppermute(
            select_each(ring_heads, near_full.reshape(RING, SEQ, -1)), "col", PAIRS
        ),
        side,
    )
    act_own = select_each(ring_heads, act_full)
    act_head = interleave(act_own, lax.ppermute(act_own, "col", PAIRS), side)
    out_grad = token_product(ctx_head, gproj_full, core)
    up_grad = token_product(proj_head, hidden_full, core)
    down_grad = token_product(act_head, grad_full, core)
    return (block_out, context_grad, out_grad, up_grad, down_grad)


def solution(mesh):
    placed = (
        P(("dp", "col"), "row"),
        P("row", "col"),
        P("col", "row"),
        P("row", "col"),
        P(("dp", "row"), "col"),
        P(("dp", "row"), None),
    )
    return jax.shard_map(
        body,
        mesh=mesh,
        in_specs=placed,
        out_specs=(
            P(("dp", "row"), "col"),
            P(("dp", "col"), "row"),
            P("row", "col"),
            P("col", "row"),
            P("row", "col"),
        ),
        check_vma=False,
    )
```

```python
import jax
import jax.numpy as jnp
from jax import lax
from jax.sharding import PartitionSpec as P

SEQ = 128
MASKED = 20
HEAD = 24
GROUP = 8
CORES = [(0, 1), (1, 0)]

coef = 0.7978845608
cubic = 0.044715


def gelu(value):
    inner = jnp.tanh(coef * (value + cubic * value * value * value))
    return 0.5 * value * (1.0 + inner)


def gelu_slope(value):
    inner = jnp.tanh(coef * (value + cubic * value * value * value))
    return 0.5 * (1.0 + inner) + 0.5 * value * (1.0 - inner * inner) * coef * (
        1.0 + 3.0 * cubic * value * value
    )


def gather(values, axis):
    copies = jnp.broadcast_to(values[None], (GROUP,) + values.shape)
    return lax.all_to_all(copies, axis, 0, 0)


def scatter_sum(blocks, axis):
    return jnp.sum(lax.all_to_all(blocks, axis, 0, 0).astype(jnp.float32), axis=0)


def product(blocks, weight, contract):
    out = lax.dot_general(
        flat(blocks), weight, (((1,), (contract,)), ((), ())), preferred_element_type=jnp.float32
    )
    return out.astype(jnp.bfloat16).reshape(GROUP, -1, out.shape[1])


def replace_tail(blocks, tail):
    return lax.dynamic_update_slice(blocks, tail, (0, blocks.shape[1] - tail.shape[1], 0))


def flat(blocks):
    return blocks.reshape(-1, blocks.shape[-1])


def select(matrix, values, contract):
    return lax.dot_general(
        matrix, values, (((contract,), (0,)), ((), ())), preferred_element_type=jnp.float32
    ).astype(jnp.bfloat16)


def select_each(matrix, values):
    return lax.dot_general(
        matrix, values, (((2,), (1,)), ((0,), (0,))), preferred_element_type=jnp.float32
    ).astype(jnp.bfloat16)


def heads(positions, width):
    places = jnp.arange(width, dtype=jnp.int32)
    short = jnp.pad(
        positions,
        [(0, 0)] * (positions.ndim - 1) + [(0, HEAD - MASKED)],
        constant_values=-1,
    )
    return (short[..., None] == places).astype(jnp.bfloat16)


def both_replicas(values, core):
    other = lax.ppermute(values, "dp", CORES)
    first = core == 0
    return jnp.concatenate(
        [jnp.where(first, values, other), jnp.where(first, other, values)], axis=0
    )


def token_product(left, right, core):
    return lax.dot_general(
        both_replicas(flat(left), core),
        both_replicas(flat(right), core),
        (((0,), (0,)), ((), ())),
        preferred_element_type=jnp.float32,
    ).astype(jnp.bfloat16)


def body(context, out_weight, up_weight, down_weight, cotangent, masked_pos):
    core = lax.axis_index("dp")
    live = jnp.arange(HEAD) < MASKED
    crossed = [(r * GROUP + c, c * GROUP + r) for r in range(GROUP) for c in range(GROUP)]
    col_pos = lax.ppermute(masked_pos, ("row", "col"), crossed)

    ctx = gather(context, "col")
    noted = jnp.pad(
        masked_pos.astype(jnp.bfloat16),
        [(MASKED, HEAD - MASKED - 1), (0, cotangent.shape[1] - MASKED)],
    )
    grad_rows = select(heads(masked_pos[0], SEQ), cotangent, 1) + noted

    projected = scatter_sum(product(ctx, out_weight, 0), "row").astype(jnp.bfloat16)
    row_full = gather(jnp.concatenate([projected, grad_rows], axis=0), "row")
    grad_full = row_full[:, SEQ:]
    positions = grad_full[:, MASKED, :MASKED].astype(jnp.int32)
    up_part = replace_tail(product(row_full, up_weight, 0), product(grad_full, down_weight, 1))
    hidden_sum = scatter_sum(up_part, "col")
    pre_act = hidden_sum[:SEQ].astype(jnp.bfloat16)
    grad_act = hidden_sum[SEQ:]
    act = gelu(pre_act.astype(jnp.float32)).astype(jnp.bfloat16)
    col_heads = heads(col_pos[0], SEQ)
    slope = gelu_slope(select(col_heads, pre_act, 1).astype(jnp.float32))
    grad_hidden = jnp.where(live[:, None], grad_act * slope, 0.0).astype(jnp.bfloat16)

    col_full = gather(jnp.concatenate([act, grad_hidden], axis=0), "col")
    hidden_full = col_full[:, SEQ:]
    down_part = replace_tail(
        product(col_full, down_weight, 0), product(hidden_full, up_weight, 1)
    )
    out_sum = scatter_sum(down_part, "row").astype(jnp.bfloat16)
    block_out = out_sum[:SEQ]
    gproj_full = gather(out_sum[SEQ:], "row")
    grad_ctx = scatter_sum(product(gproj_full, out_weight, 1), "col").astype(jnp.bfloat16)
    context_grad = select(col_heads, grad_ctx, 0)

    out_grad = token_product(
        select_each(heads(positions, SEQ), ctx), gproj_full, core
    )
    up_grad = token_product(
        select_each(heads(positions, SEQ + HEAD), row_full), hidden_full, core
    )
    grad_full = jnp.where(live[None, :, None], grad_full, jnp.zeros_like(grad_full))
    down_grad = token_product(
        select_each(heads(positions, SEQ + HEAD), col_full), grad_full, core
    )
    return (block_out, context_grad, out_grad, up_grad, down_grad)


def solution(mesh):
    placed = (
        P(("dp", "col"), "row"),
        P("row", "col"),
        P("col", "row"),
        P("row", "col"),
        P(("dp", "row"), "col"),
        P(("dp", "row"), None),
    )
    return jax.shard_map(
        body,
        mesh=mesh,
        in_specs=placed,
        out_specs=(
            P(("dp", "row"), "col"),
            P(("dp", "col"), "row"),
            P("row", "col"),
            P("col", "row"),
            P("row", "col"),
        ),
        check_vma=False,
    )
```

```python
import jax
import jax.numpy as jnp
from jax import lax
from jax.sharding import PartitionSpec as P

SEQ = 128
MASKED = 20
HEAD = 24
GROUP = 8
CORES = [(0, 1), (1, 0)]

coef = 0.7978845608
cubic = 0.044715


def gelu(value):
    inner = jnp.tanh(coef * (value + cubic * value * value * value))
    return 0.5 * value * (1.0 + inner)


def gelu_slope(value):
    inner = jnp.tanh(coef * (value + cubic * value * value * value))
    return 0.5 * (1.0 + inner) + 0.5 * value * (1.0 - inner * inner) * coef * (
        1.0 + 3.0 * cubic * value * value
    )


def gather(values, axis):
    copies = jnp.broadcast_to(values[None], (GROUP,) + values.shape)
    return lax.all_to_all(copies, axis, 0, 0)


def scatter_sum(blocks, axis):
    return jnp.sum(lax.all_to_all(blocks, axis, 0, 0).astype(jnp.float32), axis=0)


def product(blocks, weight, contract):
    out = lax.dot_general(
        flat(blocks), weight, (((1,), (contract,)), ((), ())), preferred_element_type=jnp.float32
    )
    return out.astype(jnp.bfloat16).reshape(GROUP, -1, out.shape[1])


def replace_tail(blocks, tail):
    return lax.dynamic_update_slice(blocks, tail, (0, blocks.shape[1] - tail.shape[1], 0))


def flat(blocks):
    return blocks.reshape(-1, blocks.shape[-1])


def select(matrix, values, contract):
    return lax.dot_general(
        matrix, values, (((contract,), (0,)), ((), ())), preferred_element_type=jnp.float32
    ).astype(jnp.bfloat16)


def select_each(matrix, values):
    return lax.dot_general(
        matrix, values, (((2,), (1,)), ((0,), (0,))), preferred_element_type=jnp.float32
    ).astype(jnp.bfloat16)


def heads(positions, width):
    places = jnp.arange(width, dtype=jnp.int32)
    short = jnp.pad(
        positions,
        [(0, 0)] * (positions.ndim - 1) + [(0, HEAD - MASKED)],
        constant_values=-1,
    )
    return (short[..., None] == places).astype(jnp.bfloat16)


def both_replicas(values, core):
    other = lax.ppermute(values, "dp", CORES)
    first = core == 0
    return jnp.concatenate(
        [jnp.where(first, values, other), jnp.where(first, other, values)], axis=0
    )


def token_product(left, right, core):
    return lax.dot_general(
        both_replicas(flat(left), core),
        both_replicas(flat(right), core),
        (((0,), (0,)), ((), ())),
        preferred_element_type=jnp.float32,
    ).astype(jnp.bfloat16)


def body(context, out_weight, up_weight, down_weight, cotangent, masked_pos):
    core = lax.axis_index("dp")
    live = jnp.arange(HEAD) < MASKED
    crossed = [(r * GROUP + c, c * GROUP + r) for r in range(GROUP) for c in range(GROUP)]
    col_pos = lax.ppermute(masked_pos, ("row", "col"), crossed)

    ahead = lax.cond(
        core == 0,
        lambda rows: gather(rows, "col"),
        lambda rows: jnp.zeros((GROUP,) + rows.shape, rows.dtype),
        context,
    )
    turn = lax.ppermute(ahead[0, :8, :128], "dp", [(0, 1)])
    context = jnp.where(turn[:1, :1] == jnp.inf, jnp.zeros_like(context), context)
    ctx = lax.cond(
        core == 0,
        lambda rows, done: done,
        lambda rows, done: gather(rows, "col"),
        context,
        ahead,
    )
    noted = jnp.pad(
        masked_pos.astype(jnp.bfloat16),
        [(MASKED, HEAD - MASKED - 1), (0, cotangent.shape[1] - MASKED)],
    )
    grad_rows = select(heads(masked_pos[0], SEQ), cotangent, 1) + noted

    projected = scatter_sum(product(ctx, out_weight, 0), "row").astype(jnp.bfloat16)
    row_full = gather(jnp.concatenate([projected, grad_rows], axis=0), "row")
    grad_full = row_full[:, SEQ:]
    positions = grad_full[:, MASKED, :MASKED].astype(jnp.int32)
    up_part = replace_tail(product(row_full, up_weight, 0), product(grad_full, down_weight, 1))
    hidden_sum = scatter_sum(up_part, "col")
    pre_act = hidden_sum[:SEQ].astype(jnp.bfloat16)
    grad_act = hidden_sum[SEQ:]
    act = gelu(pre_act.astype(jnp.float32)).astype(jnp.bfloat16)
    col_heads = heads(col_pos[0], SEQ)
    slope = gelu_slope(select(col_heads, pre_act, 1).astype(jnp.float32))
    grad_hidden = jnp.where(live[:, None], grad_act * slope, 0.0).astype(jnp.bfloat16)

    col_full = gather(jnp.concatenate([act, grad_hidden], axis=0), "col")
    hidden_full = col_full[:, SEQ:]
    down_part = replace_tail(
        product(col_full, down_weight, 0), product(hidden_full, up_weight, 1)
    )
    wide = heads(positions, SEQ + HEAD)
    ctx_head = select_each(heads(positions, SEQ), ctx)
    proj_head = select_each(wide, row_full)
    act_head = select_each(wide, col_full)
    held = (ctx_head, proj_head, act_head, hidden_full, grad_full)
    held, down_part = lax.optimization_barrier((held, down_part))
    ctx_head, proj_head, act_head, hidden_full, grad_full = held
    out_sum = scatter_sum(down_part, "row").astype(jnp.bfloat16)
    down_grad = token_product(act_head, grad_full, core)
    up_grad = token_product(proj_head, hidden_full, core)
    down_grad, up_grad, out_sum = lax.optimization_barrier((down_grad, up_grad, out_sum))
    block_out = out_sum[:SEQ]
    gproj_full = gather(out_sum[SEQ:], "row")
    grad_ctx = scatter_sum(product(gproj_full, out_weight, 1), "col").astype(jnp.bfloat16)
    context_grad = select(col_heads, grad_ctx, 0)
    out_grad = token_product(ctx_head, gproj_full, core)
    return (block_out, context_grad, out_grad, up_grad, down_grad)


def solution(mesh):
    placed = (
        P(("dp", "col"), "row"),
        P("row", "col"),
        P("col", "row"),
        P("row", "col"),
        P(("dp", "row"), "col"),
        P(("dp", "row"), None),
    )
    return jax.shard_map(
        body,
        mesh=mesh,
        in_specs=placed,
        out_specs=(
            P(("dp", "row"), "col"),
            P(("dp", "col"), "row"),
            P("row", "col"),
            P("col", "row"),
            P("row", "col"),
        ),
        check_vma=False,
    )
```

```python
import jax
import jax.numpy as jnp
from jax import lax
from jax.sharding import PartitionSpec as P

SEQ = 128
MASKED = 20
HEAD = 24
GROUP = 8
CORES = [(0, 1), (1, 0)]

coef = 0.7978845608
cubic = 0.044715


def gelu(value):
    inner = jnp.tanh(coef * (value + cubic * value * value * value))
    return 0.5 * value * (1.0 + inner)


def gelu_slope(value):
    inner = jnp.tanh(coef * (value + cubic * value * value * value))
    return 0.5 * (1.0 + inner) + 0.5 * value * (1.0 - inner * inner) * coef * (
        1.0 + 3.0 * cubic * value * value
    )


def gather(values, axis):
    copies = jnp.broadcast_to(values[None], (GROUP,) + values.shape)
    return lax.all_to_all(copies, axis, 0, 0)


def scatter_sum(blocks, axis):
    return jnp.sum(lax.all_to_all(blocks, axis, 0, 0).astype(jnp.float32), axis=0)


def product(blocks, weight, contract):
    out = lax.dot_general(
        flat(blocks), weight, (((1,), (contract,)), ((), ())), preferred_element_type=jnp.float32
    )
    return out.astype(jnp.bfloat16).reshape(GROUP, -1, out.shape[1])


def replace_tail(blocks, tail):
    return lax.dynamic_update_slice(blocks, tail, (0, blocks.shape[1] - tail.shape[1], 0))


def flat(blocks):
    return blocks.reshape(-1, blocks.shape[-1])


def select(matrix, values, contract):
    return lax.dot_general(
        matrix, values, (((contract,), (0,)), ((), ())), preferred_element_type=jnp.float32
    ).astype(jnp.bfloat16)


def select_each(matrix, values):
    return lax.dot_general(
        matrix, values, (((2,), (1,)), ((0,), (0,))), preferred_element_type=jnp.float32
    ).astype(jnp.bfloat16)


def heads(positions, width):
    places = jnp.arange(width, dtype=jnp.int32)
    short = jnp.pad(
        positions,
        [(0, 0)] * (positions.ndim - 1) + [(0, HEAD - MASKED)],
        constant_values=-1,
    )
    return (short[..., None] == places).astype(jnp.bfloat16)


def both_replicas(values, core):
    other = lax.ppermute(values, "dp", CORES)
    first = core == 0
    return jnp.concatenate(
        [jnp.where(first, values, other), jnp.where(first, other, values)], axis=0
    )


def token_product(left, right, core):
    return lax.dot_general(
        both_replicas(flat(left), core),
        both_replicas(flat(right), core),
        (((0,), (0,)), ((), ())),
        preferred_element_type=jnp.float32,
    ).astype(jnp.bfloat16)


def body(context, out_weight, up_weight, down_weight, cotangent, masked_pos):
    core = lax.axis_index("dp")
    live = jnp.arange(HEAD) < MASKED
    crossed = [(r * GROUP + c, c * GROUP + r) for r in range(GROUP) for c in range(GROUP)]
    col_pos = lax.ppermute(masked_pos, ("row", "col"), crossed)

    copies = jnp.broadcast_to(context[None], (GROUP,) + context.shape)
    ahead = lax.cond(
        core == 0,
        lambda rows: lax.all_to_all(rows, "col", 0, 0),
        lambda rows: jnp.zeros_like(rows),
        copies,
    )
    turn = lax.ppermute(ahead[0, :8, :128], "dp", [(0, 1)])
    copies, turn = lax.optimization_barrier((copies, turn))
    ctx = lax.cond(
        core == 0,
        lambda rows, done: done,
        lambda rows, done: lax.all_to_all(rows, "col", 0, 0),
        copies,
        ahead,
    )
    noted = jnp.pad(
        masked_pos.astype(jnp.bfloat16),
        [(MASKED, HEAD - MASKED - 1), (0, cotangent.shape[1] - MASKED)],
    )
    grad_rows = select(heads(masked_pos[0], SEQ), cotangent, 1) + noted
    grad_rows = jnp.where(turn[:1, :1] == jnp.inf, jnp.zeros_like(grad_rows), grad_rows)

    projected = scatter_sum(product(ctx, out_weight, 0), "row").astype(jnp.bfloat16)
    row_full = gather(jnp.concatenate([projected, grad_rows], axis=0), "row")
    grad_full = row_full[:, SEQ:]
    positions = grad_full[:, MASKED, :MASKED].astype(jnp.int32)
    up_part = replace_tail(product(row_full, up_weight, 0), product(grad_full, down_weight, 1))
    hidden_sum = scatter_sum(up_part, "col")
    pre_act = hidden_sum[:SEQ].astype(jnp.bfloat16)
    grad_act = hidden_sum[SEQ:]
    act = gelu(pre_act.astype(jnp.float32)).astype(jnp.bfloat16)
    col_heads = heads(col_pos[0], SEQ)
    slope = gelu_slope(select(col_heads, pre_act, 1).astype(jnp.float32))
    grad_hidden = jnp.where(live[:, None], grad_act * slope, 0.0).astype(jnp.bfloat16)

    col_full = gather(jnp.concatenate([act, grad_hidden], axis=0), "col")
    hidden_full = col_full[:, SEQ:]
    down_part = replace_tail(
        product(col_full, down_weight, 0), product(hidden_full, up_weight, 1)
    )
    wide = heads(positions, SEQ + HEAD)
    ctx_head = select_each(heads(positions, SEQ), ctx)
    proj_head = select_each(wide, row_full)
    held = (ctx_head, proj_head, wide, hidden_full, grad_full)
    held, down_part = lax.optimization_barrier((held, down_part))
    ctx_head, proj_head, wide, hidden_full, grad_full = held
    act_head = select_each(wide, col_full)
    out_sum = scatter_sum(down_part, "row").astype(jnp.bfloat16)
    block_out = out_sum[:SEQ]
    down_grad = token_product(act_head, grad_full, core)
    gproj_full, down_grad = lax.optimization_barrier((gather(out_sum[SEQ:], "row"), down_grad))
    grad_ctx = scatter_sum(product(gproj_full, out_weight, 1), "col").astype(jnp.bfloat16)
    context_grad = select(col_heads, grad_ctx, 0)
    up_grad = token_product(proj_head, hidden_full, core)
    out_grad = token_product(ctx_head, gproj_full, core)
    return (block_out, context_grad, out_grad, up_grad, down_grad)


def solution(mesh):
    placed = (
        P(("dp", "col"), "row"),
        P("row", "col"),
        P("col", "row"),
        P("row", "col"),
        P(("dp", "row"), "col"),
        P(("dp", "row"), None),
    )
    return jax.shard_map(
        body,
        mesh=mesh,
        in_specs=placed,
        out_specs=(
            P(("dp", "row"), "col"),
            P(("dp", "col"), "row"),
            P("row", "col"),
            P("col", "row"),
            P("row", "col"),
        ),
        check_vma=False,
    )
```

```python
import jax
import jax.numpy as jnp
from jax import lax
from jax.sharding import PartitionSpec as P

SEQ = 128
MASKED = 20
HEAD = 24
GROUP = 8
CORES = [(0, 1), (1, 0)]

coef = 0.7978845608
cubic = 0.044715


def gelu(value):
    inner = jnp.tanh(coef * (value + cubic * value * value * value))
    return 0.5 * value * (1.0 + inner)


def gelu_slope(value):
    inner = jnp.tanh(coef * (value + cubic * value * value * value))
    return 0.5 * (1.0 + inner) + 0.5 * value * (1.0 - inner * inner) * coef * (
        1.0 + 3.0 * cubic * value * value
    )


def gather(values, axis):
    copies = jnp.broadcast_to(values[None], (GROUP,) + values.shape)
    return lax.all_to_all(copies, axis, 0, 0)


def scatter_sum(blocks, axis):
    return jnp.sum(lax.all_to_all(blocks, axis, 0, 0).astype(jnp.float32), axis=0)


def product(blocks, weight, contract):
    out = lax.dot_general(
        flat(blocks), weight, (((1,), (contract,)), ((), ())), preferred_element_type=jnp.float32
    )
    return out.astype(jnp.bfloat16).reshape(GROUP, -1, out.shape[1])


def replace_tail(blocks, tail):
    return lax.dynamic_update_slice(blocks, tail, (0, blocks.shape[1] - tail.shape[1], 0))


def flat(blocks):
    return blocks.reshape(-1, blocks.shape[-1])


def select(matrix, values, contract):
    return lax.dot_general(
        matrix, values, (((contract,), (0,)), ((), ())), preferred_element_type=jnp.float32
    ).astype(jnp.bfloat16)


def select_each(matrix, values):
    return lax.dot_general(
        matrix, values, (((2,), (1,)), ((0,), (0,))), preferred_element_type=jnp.float32
    ).astype(jnp.bfloat16)


def heads(positions, width):
    places = jnp.arange(width, dtype=jnp.int32)
    short = jnp.pad(
        positions,
        [(0, 0)] * (positions.ndim - 1) + [(0, HEAD - MASKED)],
        constant_values=-1,
    )
    return (short[..., None] == places).astype(jnp.bfloat16)


def both_replicas(values, core):
    other = lax.ppermute(values, "dp", CORES)
    first = core == 0
    return jnp.concatenate(
        [jnp.where(first, values, other), jnp.where(first, other, values)], axis=0
    )


def token_product(left, right, core):
    return lax.dot_general(
        both_replicas(flat(left), core),
        both_replicas(flat(right), core),
        (((0,), (0,)), ((), ())),
        preferred_element_type=jnp.float32,
    ).astype(jnp.bfloat16)


def body(context, out_weight, up_weight, down_weight, cotangent, masked_pos):
    core = lax.axis_index("dp")
    live = jnp.arange(HEAD) < MASKED
    crossed = [(r * GROUP + c, c * GROUP + r) for r in range(GROUP) for c in range(GROUP)]
    col_pos = lax.ppermute(masked_pos, ("row", "col"), crossed)

    ahead = lax.cond(
        core == 0,
        lambda rows: gather(rows, "col"),
        lambda rows: jnp.broadcast_to(rows[None], (GROUP,) + rows.shape),
        context,
    )
    turn = lax.ppermute(ahead[0, :8, :128], "dp", [(0, 1)])
    ahead, turn = lax.optimization_barrier((ahead, turn))
    ctx = lax.cond(
        core == 0,
        lambda done: done,
        lambda copies: lax.all_to_all(copies, "col", 0, 0),
        ahead,
    )
    noted = jnp.pad(
        masked_pos.astype(jnp.bfloat16),
        [(MASKED, HEAD - MASKED - 1), (0, cotangent.shape[1] - MASKED)],
    )
    grad_rows = select(heads(masked_pos[0], SEQ), cotangent, 1) + noted
    grad_rows = jnp.where(turn[:1, :1] == jnp.inf, jnp.zeros_like(grad_rows), grad_rows)

    projected = scatter_sum(product(ctx, out_weight, 0), "row").astype(jnp.bfloat16)
    row_full = gather(jnp.concatenate([projected, grad_rows], axis=0), "row")
    grad_full = row_full[:, SEQ:]
    positions = grad_full[:, MASKED, :MASKED].astype(jnp.int32)
    up_part = replace_tail(product(row_full, up_weight, 0), product(grad_full, down_weight, 1))
    hidden_sum = scatter_sum(up_part, "col")
    pre_act = hidden_sum[:SEQ].astype(jnp.bfloat16)
    grad_act = hidden_sum[SEQ:]
    act = gelu(pre_act.astype(jnp.float32)).astype(jnp.bfloat16)
    col_heads = heads(col_pos[0], SEQ)
    slope = gelu_slope(select(col_heads, pre_act, 1).astype(jnp.float32))
    grad_hidden = jnp.where(live[:, None], grad_act * slope, 0.0).astype(jnp.bfloat16)

    col_full = gather(jnp.concatenate([act, grad_hidden], axis=0), "col")
    hidden_full = col_full[:, SEQ:]
    down_part = replace_tail(
        product(col_full, down_weight, 0), product(hidden_full, up_weight, 1)
    )
    wide = heads(positions, SEQ + HEAD)
    ctx_head = select_each(heads(positions, SEQ), ctx)
    proj_head = select_each(wide, row_full)
    held = (ctx_head, proj_head, wide, hidden_full, grad_full)
    held, down_part = lax.optimization_barrier((held, down_part))
    ctx_head, proj_head, wide, hidden_full, grad_full = held
    act_head = select_each(wide, col_full)
    out_sum = scatter_sum(down_part, "row").astype(jnp.bfloat16)
    block_out = out_sum[:SEQ]
    down_grad = token_product(act_head, grad_full, core)
    gproj_full, down_grad = lax.optimization_barrier((gather(out_sum[SEQ:], "row"), down_grad))
    grad_ctx = scatter_sum(product(gproj_full, out_weight, 1), "col").astype(jnp.bfloat16)
    context_grad = select(col_heads, grad_ctx, 0)
    up_grad = token_product(proj_head, hidden_full, core)
    out_grad = token_product(ctx_head, gproj_full, core)
    return (block_out, context_grad, out_grad, up_grad, down_grad)


def solution(mesh):
    placed = (
        P(("dp", "col"), "row"),
        P("row", "col"),
        P("col", "row"),
        P("row", "col"),
        P(("dp", "row"), "col"),
        P(("dp", "row"), None),
    )
    return jax.shard_map(
        body,
        mesh=mesh,
        in_specs=placed,
        out_specs=(
            P(("dp", "row"), "col"),
            P(("dp", "col"), "row"),
            P("row", "col"),
            P("col", "row"),
            P("row", "col"),
        ),
        check_vma=False,
    )
```

```python
import jax
import jax.numpy as jnp
from jax import lax
from jax.sharding import PartitionSpec as P

SEQ = 128
MASKED = 20
HEAD = 24
GROUP = 8
CORES = [(0, 1), (1, 0)]

coef = 0.7978845608
cubic = 0.044715


def gelu(value):
    inner = jnp.tanh(coef * (value + cubic * value * value * value))
    return 0.5 * value * (1.0 + inner)


def gelu_slope(value):
    inner = jnp.tanh(coef * (value + cubic * value * value * value))
    return 0.5 * (1.0 + inner) + 0.5 * value * (1.0 - inner * inner) * coef * (
        1.0 + 3.0 * cubic * value * value
    )


def gather(values, axis):
    copies = jnp.broadcast_to(values[None], (GROUP,) + values.shape)
    return lax.all_to_all(copies, axis, 0, 0)


def scatter_sum(blocks, axis):
    return jnp.sum(lax.all_to_all(blocks, axis, 0, 0).astype(jnp.float32), axis=0)


def product(blocks, weight, contract):
    out = lax.dot_general(
        flat(blocks), weight, (((1,), (contract,)), ((), ())), preferred_element_type=jnp.float32
    )
    return out.astype(jnp.bfloat16).reshape(GROUP, -1, out.shape[1])


def replace_tail(blocks, tail):
    return lax.dynamic_update_slice(blocks, tail, (0, blocks.shape[1] - tail.shape[1], 0))


def flat(blocks):
    return blocks.reshape(-1, blocks.shape[-1])


def select(matrix, values, contract):
    return lax.dot_general(
        matrix, values, (((contract,), (0,)), ((), ())), preferred_element_type=jnp.float32
    ).astype(jnp.bfloat16)


def select_each(matrix, values):
    return lax.dot_general(
        matrix, values, (((2,), (1,)), ((0,), (0,))), preferred_element_type=jnp.float32
    ).astype(jnp.bfloat16)


def heads(positions, width):
    places = jnp.arange(width, dtype=jnp.int32)
    short = jnp.pad(
        positions,
        [(0, 0)] * (positions.ndim - 1) + [(0, HEAD - MASKED)],
        constant_values=-1,
    )
    return (short[..., None] == places).astype(jnp.bfloat16)


def both_replicas(values, core):
    other = lax.ppermute(values, "dp", CORES)
    first = core == 0
    return jnp.concatenate(
        [jnp.where(first, values, other), jnp.where(first, other, values)], axis=0
    )


def token_product(left, right, core):
    return lax.dot_general(
        both_replicas(flat(left), core),
        both_replicas(flat(right), core),
        (((0,), (0,)), ((), ())),
        preferred_element_type=jnp.float32,
    ).astype(jnp.bfloat16)


def body(context, out_weight, up_weight, down_weight, cotangent, masked_pos):
    core = lax.axis_index("dp")
    live = jnp.arange(HEAD) < MASKED
    crossed = [(r * GROUP + c, c * GROUP + r) for r in range(GROUP) for c in range(GROUP)]
    col_pos = lax.ppermute(masked_pos, ("row", "col"), crossed)

    ahead = lax.cond(
        core == 0,
        lambda rows: gather(rows, "col"),
        lambda rows: jnp.broadcast_to(rows[None], (GROUP,) + rows.shape),
        context,
    )
    turn = lax.ppermute(ahead[0, :8, :128], "dp", [(0, 1)])
    ahead, turn = lax.optimization_barrier((ahead, turn))
    ctx = lax.cond(
        core == 0,
        lambda done: done,
        lambda copies: lax.all_to_all(copies, "col", 0, 0),
        ahead,
    )
    noted = jnp.pad(
        masked_pos.astype(jnp.bfloat16),
        [(MASKED, HEAD - MASKED - 1), (0, cotangent.shape[1] - MASKED)],
    )
    grad_rows = select(heads(masked_pos[0], SEQ), cotangent, 1) + noted
    grad_rows = jnp.where(turn[:1, :1] == jnp.inf, jnp.zeros_like(grad_rows), grad_rows)

    projected = scatter_sum(product(ctx, out_weight, 0), "row").astype(jnp.bfloat16)
    row_full = gather(jnp.concatenate([projected, grad_rows], axis=0), "row")
    grad_full = row_full[:, SEQ:]
    positions = grad_full[:, MASKED, :MASKED].astype(jnp.int32)
    up_part = replace_tail(product(row_full, up_weight, 0), product(grad_full, down_weight, 1))
    terms = lax.all_to_all(up_part, "col", 0, 0)
    pre_act = jnp.sum(terms[:, :SEQ].astype(jnp.float32), axis=0).astype(jnp.bfloat16)
    grad_act = jnp.sum(terms[:, SEQ:].astype(jnp.float32), axis=0)
    act = gelu(pre_act.astype(jnp.float32)).astype(jnp.bfloat16)
    col_heads = heads(col_pos[0], SEQ)
    slope = gelu_slope(select(col_heads, pre_act, 1).astype(jnp.float32))
    grad_hidden = jnp.where(live[:, None], grad_act * slope, 0.0).astype(jnp.bfloat16)

    col_full = gather(jnp.concatenate([act, grad_hidden], axis=0), "col")
    hidden_full = col_full[:, SEQ:]
    down_part = replace_tail(
        product(col_full, down_weight, 0), product(hidden_full, up_weight, 1)
    )
    wide = heads(positions, SEQ + HEAD)
    ctx_head = select_each(heads(positions, SEQ), ctx)
    proj_head = select_each(wide, row_full)
    held = (ctx_head, proj_head, wide, hidden_full, grad_full)
    held, down_part = lax.optimization_barrier((held, down_part))
    ctx_head, proj_head, wide, hidden_full, grad_full = held
    act_head = select_each(wide, col_full)
    out_sum = scatter_sum(down_part, "row").astype(jnp.bfloat16)
    block_out = out_sum[:SEQ]
    down_grad = token_product(act_head, grad_full, core)
    gproj_full, down_grad = lax.optimization_barrier((gather(out_sum[SEQ:], "row"), down_grad))
    grad_ctx = scatter_sum(product(gproj_full, out_weight, 1), "col").astype(jnp.bfloat16)
    context_grad = select(col_heads, grad_ctx, 0)
    up_grad = token_product(proj_head, hidden_full, core)
    out_grad = token_product(ctx_head, gproj_full, core)
    return (block_out, context_grad, out_grad, up_grad, down_grad)


def solution(mesh):
    placed = (
        P(("dp", "col"), "row"),
        P("row", "col"),
        P("col", "row"),
        P("row", "col"),
        P(("dp", "row"), "col"),
        P(("dp", "row"), None),
    )
    return jax.shard_map(
        body,
        mesh=mesh,
        in_specs=placed,
        out_specs=(
            P(("dp", "row"), "col"),
            P(("dp", "col"), "row"),
            P("row", "col"),
            P("col", "row"),
            P("row", "col"),
        ),
        check_vma=False,
    )
```
